256 devices in a mesh: blk: 128 (over x, z, y_hi, core), panel: 2 (over y_lo).
Axes of the slice: x: 4, y: 4 (y_hi: 2, y_lo: 2; y = y_hi * 2 + y_lo), z: 8, core: 2. Of those that a mesh axis runs over, the one named last changes fastest.
Arguments:
- tiles: bfloat16 [131072, 2, 8, 256], P('blk', 'panel'), may hold values from -6 to 6
- loadings: float32 [131072, 512], P('blk'), may hold values from -6 to 6
- maps: float32 [128, 2, 256, 512], P('blk', 'panel'), may hold values from -6 to 6
- run_counts: int32 [512], P('blk'), may hold values from 64 to 256, as said below
Outputs:
- loadings_out: float32 [131072, 512], P(('blk', 'panel'))
- maps_after: float32 [128, 2, 256, 512], P('blk', 'panel')
The draws below stay inside these ranges and needn't reach their ends.
Inputs may be any that keep to these rules, and one draw needn't show every extreme that they name: `run_counts`: valid frames at the start of each run of 256 frames; some run has all 256 valid and some only 64.
All inputs are finite; a program needn't handle non-finite values.
Results may differ from the reference program's by a relative error of at most 0.0028.
Values may be sent and summed in bfloat16 or wider, within the bound.
No kernel may reach another device: no remote copies, remote signals or barrier semaphores. Data moves between devices by JAX's collectives and lax.ppermute only.
A program may use at most 64 MiB of HBM per device.

```python
import jax
import jax.numpy as jnp
from jax import lax

R = 512
G = 256
RUN_LEN = 256
RUNS_DEV = 4
STEPS = 8
FRAMES_DEV = 1024
FRAMES = 131072
N_BLK = 128
N_PANEL = 2


def draw_run_counts(key, part):
    total = N_BLK * RUNS_DEV
    first, second, third = jax.random.split(jax.random.fold_in(key, 17), 3)
    values = jax.random.randint(first, (total,), RUN_LEN // 4, RUN_LEN + 1)
    place = jax.random.randint(second, (), 0, total)
    other = (place + 1 + jax.random.randint(third, (), 0, total - 1)) % total
    values = values.at[place].set(RUN_LEN)
    values = values.at[other].set(RUN_LEN // 4)
    return values.astype(jnp.int32)


def factor_draw(key, rows, width):
    first = jax.random.fold_in(key, 0)
    values = jax.random.normal(first, (rows, width), jnp.float32)
    return jnp.clip(values, -6.0, 6.0)


def draw_loadings(key, part):
    values = factor_draw(jax.random.fold_in(key, 23), FRAMES, R)
    return values.astype(jnp.float32)


def draw_maps(key, part):
    values = factor_draw(jax.random.fold_in(key, 29), N_BLK * N_PANEL * G, R)
    return values.reshape(N_BLK, N_PANEL, G, R).astype(jnp.float32)


def shard_levels(own_key, shape, cuts, least, largest):
    def one(dim, shards_of):
        heights = jax.random.uniform(jax.random.fold_in(jax.random.fold_in(own_key, 6), dim), (shards_of,), jnp.float32, least / len(cuts), largest / len(cuts))
        return jnp.repeat(jnp.exp(heights), shape[dim] // shards_of).reshape((-1,) + (1,) * (len(shape) - dim - 1))

    factor_of = one(*cuts[0])
    for cut in cuts[1:]:
        factor_of = factor_of * one(*cut)
    return factor_of


def bell_draw(rng, shape, spread, most, cuts=(), kind=jnp.bfloat16):
    drawn = spread * jax.random.normal(rng, shape, jnp.float32)
    if cuts:
        drawn = drawn * shard_levels(rng, shape, cuts, -0.22, 0.18)
    return jnp.clip(drawn, -most, most).astype(kind)


def setup_inputs(seed: int = 0) -> dict:
    splits = jax.random.split(jax.random.key(seed), 5)
    return {
        "tiles": bell_draw(splits[0], (FRAMES, N_PANEL, STEPS, G), 1.0, 6.0, ((0, 128), (1, 2))),
        "loadings": draw_loadings(jax.random.fold_in(splits[4], 71), 0),
        "maps": draw_maps(jax.random.fold_in(splits[4], 71), 0),
        "run_counts": draw_run_counts(jax.random.fold_in(splits[4], 71), 0),
    }


map_rate = 0.1
load_rate = 0.05


def reference(tiles, loadings, maps, run_counts):
    scale = 1.0 / (R ** 0.5)
    runs = run_counts.reshape(N_BLK, RUNS_DEV)
    within = jnp.arange(FRAMES_DEV, dtype=jnp.int32)
    limits = jnp.repeat(runs, RUN_LEN, axis=1)
    mask = ((within % RUN_LEN)[None, :] < limits).astype(jnp.float32)
    current = loadings.reshape(N_BLK, FRAMES_DEV, R)
    data = tiles.reshape(N_BLK, FRAMES_DEV, N_PANEL, STEPS, G)
    held = maps
    half = STEPS // 2
    for part in range(2):
        loads_bf = current.astype(jnp.bfloat16)
        acc = jnp.zeros((N_BLK, FRAMES_DEV, R), jnp.float32)
        for step in range(part * half, (part + 1) * half):
            def one(items):
                tile, lb, block, rows = items
                xs = tile[:, :, step, :].astype(jnp.float32)
                bb = block.astype(jnp.bfloat16).astype(jnp.float32)
                lf = lb.astype(jnp.float32)
                prod = jnp.einsum('fr,pgr->fpg', lf, bb)
                resid = ((xs - prod * scale) * rows[:, None, None]).astype(jnp.bfloat16).astype(jnp.float32)
                grad_map = jnp.einsum('fpg,fr->pgr', resid, lf) * scale
                grad_load = jnp.einsum('fpg,pgr->fr', resid, bb) * scale
                return block + map_rate * grad_map, grad_load
            held, grads = lax.map(one, (data, loads_bf, held, mask))
            acc = acc + grads
            held = jnp.roll(held, 1, axis=0)
        current = current + load_rate * acc
    return current.reshape(FRAMES, R), held
```

```python
import jax
import jax.numpy as jnp
from jax import lax
from jax.experimental import pallas as pl
from jax.experimental.pallas import tpu as pltpu
from jax.sharding import PartitionSpec as P

RUN_LEN = 256
STEPS = 8

map_rate = 0.1
load_rate = 0.05

SPAN = 240.0
TOP_ROWS = 16
TINY = 1e-30

VMEM = pl.BlockSpec(memory_space=pltpu.VMEM)
SMEM = pl.BlockSpec(memory_space=pltpu.SMEM)
f32 = jnp.float32
bf16 = jnp.bfloat16


def local_call(body, small, arrays, outs, *, name, aliases=None, temp_mib=12):
    arrays = [pltpu.with_memory_space_constraint(x, pltpu.VMEM) for x in arrays]
    result = pl.pallas_call(
        body,
        in_specs=[SMEM] * len(small) + [VMEM] * len(arrays),
        out_specs=[VMEM] * len(outs),
        out_shape=[pltpu.VMEM(shape, dtype) for shape, dtype in outs],
        input_output_aliases=aliases or {},
        compiler_params=pltpu.CompilerParams(vmem_limit_bytes=temp_mib * 2**20),
        name=name,
    )(*small, *arrays)
    return result


def encode(block, out_ref):
    rank = block.shape[0]
    size = jnp.abs(block)
    top = jnp.max(size, axis=0, keepdims=True)
    top = jnp.maximum(top * (1.0 + 2.0**-6), TINY).astype(bf16)
    wide = top.astype(f32)
    code = jnp.exp2(size * (SPAN / wide) - SPAN / 2)
    out_ref[0:rank, :] = jnp.where(block < 0, -code, code).astype(bf16)
    out_ref[rank : rank + TOP_ROWS, :] = jnp.broadcast_to(top, (TOP_ROWS, block.shape[1]))


def decode(in_ref):
    rank = in_ref.shape[0] - TOP_ROWS
    code = in_ref[0:rank, :].astype(f32)
    top = in_ref[rank : rank + 1, :].astype(f32)
    size = (jnp.log2(jnp.abs(code)) + SPAN / 2) * (top / SPAN)
    return jnp.where(code < 0, -size, size)


def add_pending(acc_ref, pending, fresh):
    first = fresh
    for resid_ref, block_ref in pending:
        part = lax.dot_general(
            resid_ref[...], block_ref[...], (((1,), (1,)), ((), ())), preferred_element_type=f32
        )
        acc_ref[...] = part if first else acc_ref[...] + part
        first = False


def step_call(core, counts, block, tile, loads, loads_t, acc, pending, *, active, fresh, coded, name):
    frames, rank = loads.shape
    width = tile.shape[1]
    scale = 1.0 / rank**0.5
    n_pend = len(pending)
    has_acc = acc is not None

    def body(*refs):
        core_ref, counts_ref, block_ref, tile_ref, loads_ref, loads_t_ref = refs[:6]
        at = 6
        pend = [(refs[at + 2 * i], refs[at + 2 * i + 1]) for i in range(n_pend)]
        at += 2 * n_pend + (1 if has_acc else 0)
        out_ref, resid_ref, bb_ref, acc_ref = refs[at : at + 4]

        @pl.when(core_ref[0] == active)
        def _():
            held = decode(block_ref) if coded else block_ref[...]
            bb = held.astype(bf16)
            bb_ref[...] = bb
            rows = lax.broadcasted_iota(jnp.int32, (RUN_LEN, width), 0)
            for run in range(frames // RUN_LEN):
                at = slice(run * RUN_LEN, (run + 1) * RUN_LEN)
                prod = jnp.dot(loads_ref[at, :], bb, preferred_element_type=f32)
                diff = tile_ref[at, :].astype(f32) - prod * scale
                resid_ref[at, :] = jnp.where(rows < counts_ref[run], diff, 0.0).astype(bf16)
            grad = jnp.dot(loads_t_ref[...], resid_ref[...], preferred_element_type=f32)
            encode(held + (map_rate * scale) * grad, out_ref)

        if n_pend:

            @pl.when(core_ref[0] != active)
            def _():
                add_pending(acc_ref, pend, fresh)

    flat = [x for pair in pending for x in pair]
    arrays = [block, tile, loads, loads_t, *flat] + ([acc] if has_acc else [])
    outs = [
        ((rank + TOP_ROWS, width), bf16),
        ((frames, width), bf16),
        ((rank, width), bf16),
        ((frames, rank), f32),
    ]
    aliases = {len(arrays) + 1: 3} if has_acc else {}
    return local_call(body, [core, counts], arrays, outs, name=name, aliases=aliases)


def gather_call(core, acc, pending, start, rows, *, active, name):
    frames, rank = acc.shape

    def body(core_ref, start_ref, resid_ref, bb_ref, acc_in_ref, out_ref, acc_ref):
        @pl.when(core_ref[0] == active)
        def _():
            add_pending(acc_ref, [(resid_ref, bb_ref)], False)

        if rows == frames:
            out_ref[...] = acc_ref[...].astype(bf16)
        else:
            first = pl.multiple_of(start_ref[0] * rows, rows)
            out_ref[...] = acc_ref[pl.ds(first, rows), :].astype(bf16)

    outs = [((rows, rank), bf16), ((frames, rank), f32)]
    return local_call(body, [core, start], [*pending, acc], outs, name=name, aliases={4: 1})


def update_call(loadings, acc, arrived, *, name):
    frames, rank = acc.shape
    factor = load_rate / rank**0.5

    def body(loadings_ref, acc_ref, arrived_ref, loads_ref, loads_t_ref):
        for at in range(0, frames, RUN_LEN):
            rows = slice(at, at + RUN_LEN)
            new = loadings_ref[rows, :] + factor * (acc_ref[rows, :] + arrived_ref[rows, :].astype(f32))
            new = new.astype(bf16)
            loads_ref[rows, :] = new
            loads_t_ref[:, rows] = new.T

    outs = [((frames, rank), bf16), ((rank, frames), bf16)]
    return local_call(body, [], [loadings, acc, arrived], outs, name=name)


def first_call(loadings, maps, *, name):
    frames, rank = loadings.shape

    def body(loadings_ref, maps_ref, loads_ref, loads_t_ref, block_ref):
        for at in range(0, frames, RUN_LEN):
            rows = slice(at, at + RUN_LEN)
            new = loadings_ref[rows, :].astype(bf16)
            loads_ref[rows, :] = new
            loads_t_ref[:, rows] = new.T
        block_ref[...] = maps_ref[...].T

    outs = [((frames, rank), bf16), ((rank, frames), bf16), ((rank, maps.shape[0]), f32)]
    return local_call(body, [], [loadings, maps], outs, name=name)


def final_call(panel, loadings, acc, arrived, *, name):
    rows, rank = arrived.shape
    factor = load_rate / rank**0.5

    def body(panel_ref, loadings_ref, acc_ref, arrived_ref, out_ref):
        own = pl.ds(pl.multiple_of(panel_ref[0] * rows, rows), rows)
        out_ref[...] = loadings_ref[own, :] + factor * (
            acc_ref[own, :] + arrived_ref[...].astype(f32)
        )

    return local_call(body, [panel], [loadings, acc, arrived], [((rows, rank), f32)], name=name)[0]


def maps_call(core, block_a, block_b, *, name):
    rank = block_a.shape[0] - TOP_ROWS
    width = block_a.shape[1]

    def body(core_ref, a_ref, b_ref, out_ref):
        @pl.when(core_ref[0] == 0)
        def _():
            out_ref[...] = decode(a_ref).T

        @pl.when(core_ref[0] == 1)
        def _():
            out_ref[...] = decode(b_ref).T

    return local_call(body, [core], [block_a, block_b], [((width, rank), f32)], name=name)[0]


def per_device(tiles, loadings, maps, run_counts):
    frames, rank = loadings.shape
    n_blk = lax.axis_size("blk")
    n_panel = lax.axis_size("panel")
    core = (lax.axis_index("blk") % 2).astype(jnp.int32).reshape(1)
    panel = lax.axis_index("panel").astype(jnp.int32).reshape(1)
    other = n_panel - 1 - panel

    def hop(payload, from_core):
        pairs = [(i, (i + 1) % n_blk) for i in range(n_blk) if i % 2 == from_core]
        return lax.ppermute(payload, "blk", pairs)

    def swap(payload):
        return lax.ppermute(payload, "panel", [(i, n_panel - 1 - i) for i in range(n_panel)])

    tile = [tiles[:, 0, s, :] for s in range(STEPS)]
    loads, loads_t, block = first_call(loadings, maps[0, 0], name="first")
    chain = [block, block]
    acc = None
    half = STEPS // 2
    last = [None, None]
    for step in range(STEPS):
        for which in range(2):
            active = (step + which) % 2
            pending = []
            if which == 1:
                pending = ([] if step % half == 0 else [last[1]]) + [last[0]]
            payload, resid, bb, acc = step_call(
                core,
                run_counts,
                chain[which],
                tile[step],
                loads,
                loads_t,
                acc,
                pending,
                active=active,
                fresh=step < 2,
                coded=step > 0,
                name=f"step{step}{'EO'[which]}",
            )
            last[which] = (resid, bb)
            with jax.named_scope(f"hop{step}{'EO'[which]}"):
                chain[which] = hop(payload, active)
        if step == half - 1:
            mine, acc = gather_call(
                core, acc, last[1], other, frames, active=0, name="gather_mid"
            )
            with jax.named_scope("swap_mid"):
                arrived = swap(mine)
            loads, loads_t = update_call(loadings, acc, arrived, name="update")
    mine, acc = gather_call(
        core, acc, last[1], other, frames // n_panel, active=0, name="gather_end"
    )
    with jax.named_scope("swap_end"):
        arrived = swap(mine)
    maps_after = maps_call(core, chain[0], chain[1], name="maps_after")
    loadings_out = final_call(panel, loadings, acc, arrived, name="loadings_out")
    return loadings_out, maps_after.reshape(maps.shape)


def solution(mesh):
    in_specs = (
        P("blk", "panel", None, None),
        P("blk", None),
        P("blk", "panel", None, None),
        P("blk"),
    )
    out_specs = (P(("blk", "panel"), None), P("blk", "panel", None, None))
    return jax.shard_map(
        per_device, mesh=mesh, in_specs=in_specs, out_specs=out_specs, check_vma=False
    )
```

```python
import jax
import jax.numpy as jnp
from jax import lax
from jax.experimental import pallas as pl
from jax.experimental.pallas import tpu as pltpu
from jax.sharding import PartitionSpec as P

RUN_LEN = 256
STEPS = 8

map_rate = 0.1
load_rate = 0.05

SPAN = 240.0
TOP_ROWS = 16
TINY = 1e-30

VMEM = pl.BlockSpec(memory_space=pltpu.VMEM)
SMEM = pl.BlockSpec(memory_space=pltpu.SMEM)
f32 = jnp.float32
bf16 = jnp.bfloat16


class Calls:
    def __init__(self):
        self.token = None

    def __call__(self, body, small, arrays, outs, *, name, aliases=None, temp_mib=8):
        first = self.token is None
        n_in = len(small) + len(arrays) + (0 if first else 1)

        def wrapped(*refs):
            ins = refs[: len(small) + len(arrays)]
            body(*ins, *refs[n_in : n_in + len(outs)])

        passed = list(arrays) + ([] if first else [self.token])
        passed = [pltpu.with_memory_space_constraint(x, pltpu.VMEM) for x in passed]
        aliases = dict(aliases or {})
        if not first:
            aliases[n_in - 1] = len(outs)
        results = pl.pallas_call(
            wrapped,
            in_specs=[SMEM] * len(small) + [VMEM] * len(passed),
            out_specs=[VMEM] * (len(outs) + 1),
            out_shape=[pltpu.VMEM(shape, dtype) for shape, dtype in outs]
            + [pltpu.VMEM((8, 128), f32)],
            input_output_aliases=aliases,
            compiler_params=pltpu.CompilerParams(vmem_limit_bytes=temp_mib * 2**20),
            name=name,
        )(*small, *passed)
        self.token = results[-1]
        return results[:-1]


def encode(block, write):
    size = jnp.abs(block)
    top = jnp.max(size, axis=0, keepdims=True)
    top = jnp.maximum(top * (1.0 + 2.0**-6), TINY).astype(bf16)
    code = jnp.exp2(size * (SPAN / top.astype(f32)) - SPAN / 2)
    write(jnp.where(block < 0, -code, code).astype(bf16), top)


def into(ref):
    rank = ref.shape[0] - TOP_ROWS

    def write(codes, top):
        ref[0:rank, :] = codes
        ref[rank : rank + TOP_ROWS, :] = jnp.broadcast_to(top, (TOP_ROWS, top.shape[1]))

    return write


def decode(payload):
    rank = payload.shape[0] - TOP_ROWS
    code = payload[0:rank, :].astype(f32)
    top = payload[rank : rank + 1, :].astype(f32)
    size = (jnp.log2(jnp.abs(code)) + SPAN / 2) * (top / SPAN)
    return jnp.where(code < 0, -size, size)


def visit(held, tile_rows, counts_ref, loads_ref, loads_t_ref, resid_ref, bb_ref):
    frames, rank = loads_ref.shape
    width = held.shape[1]
    scale = 1.0 / rank**0.5
    bb = held.astype(bf16)
    bb_ref[...] = bb
    rows = lax.broadcasted_iota(jnp.int32, (RUN_LEN, width), 0)
    for run in range(frames // RUN_LEN):
        at = slice(run * RUN_LEN, (run + 1) * RUN_LEN)
        prod = jnp.dot(loads_ref[at, :], bb, preferred_element_type=f32)
        diff = tile_rows(at).astype(f32) - prod * scale
        resid_ref[at, :] = jnp.where(rows < counts_ref[run], diff, 0.0).astype(bf16)
    grad = jnp.dot(loads_t_ref[...], resid_ref[...], preferred_element_type=f32)
    return held + (map_rate * scale) * grad


def pull(resid_ref, bb_ref):
    return lax.dot_general(
        resid_ref[...], bb_ref[...], (((1,), (1,)), ((), ())), preferred_element_type=f32
    )


def per_device(tiles, loadings, maps, run_counts):
    frames, rank = loadings.shape
    width = maps.shape[2]
    half_w = width // 2
    half_f = frames // 2
    n_blk = lax.axis_size("blk")
    n_panel = lax.axis_size("panel")
    core = (lax.axis_index("blk") % 2).astype(jnp.int32).reshape(1)
    panel = lax.axis_index("panel").astype(jnp.int32).reshape(1)
    factor = load_rate / rank**0.5
    call = Calls()

    def hop(x, name):
        with jax.named_scope(name):
            return lax.ppermute(x, "blk", [(i, (i + 2) % n_blk) for i in range(n_blk)])

    def swap(x, name):
        with jax.named_scope(name):
            return lax.ppermute(x, "blk", [(i, i ^ 1) for i in range(n_blk)])

    def across(x, name):
        with jax.named_scope(name):
            return lax.ppermute(x, "panel", [(i, n_panel - 1 - i) for i in range(n_panel)])

    def at_half(index, size):
        return pl.ds(pl.multiple_of(index * size, size), size)

    payload_shape = ((rank + TOP_ROWS, half_w), bf16)
    resid_shape = ((frames, half_w), bf16)
    bb_shape = ((rank, half_w), bf16)
    acc_shape = ((frames, rank), f32)
    loads_shape = ((frames, rank), bf16)
    loads_t_shape = ((rank, frames), bf16)
    rows_shape = ((half_f, rank), bf16)

    by_step = jnp.transpose(tiles, (1, 2, 0, 3)).reshape(STEPS, frames, width)

    def first(core_ref, loadings_ref, maps_ref, loads_ref, loads_t_ref, block_ref, rows_ref):
        for at in range(0, frames, RUN_LEN):
            rows = slice(at, at + RUN_LEN)
            new = loadings_ref[rows, :].astype(bf16)
            loads_ref[rows, :] = new
            loads_t_ref[:, rows] = new.T
        block_ref[...] = maps_ref[...].T
        rows_ref[...] = loadings_ref[at_half(1 - core_ref[0], half_f), :]

    own, own_t, block, rows_out = call(
        first,
        [core],
        [loadings, maps[0, 0]],
        [loads_shape, loads_t_shape, ((rank, width), f32), ((half_f, rank), f32)],
        name="first",
    )
    other = swap(own, "swap_loads")
    other_rows = swap(rows_out, "swap_rows")
    other_counts = swap(run_counts, "swap_counts")

    def start(core_ref, counts_ref, block_ref, tile_ref, loads_ref, loads_t_ref, keep_ref, send_ref, resid_ref, bb_ref):
        new = visit(
            block_ref[...], lambda at: tile_ref[0, at, :], counts_ref, loads_ref, loads_t_ref, resid_ref, bb_ref
        )

        def write(codes, top):
            low, high = (codes[:, :half_w], top[:, :half_w]), (codes[:, half_w:], top[:, half_w:])

            @pl.when(core_ref[0] == 0)
            def _():
                into(keep_ref)(*low)
                into(send_ref)(*high)

            @pl.when(core_ref[0] == 1)
            def _():
                into(keep_ref)(*high)
                into(send_ref)(*low)

        encode(new, write)

    keep, send, resid_0, bb_0 = call(
        start,
        [core, run_counts],
        [block, by_step, own, own_t],
        [payload_shape, payload_shape, ((frames, width), bf16), ((rank, width), bf16)],
        name="step0",
    )
    came = swap(send, "swap_step0")

    def cut(core_ref, tile_ref, send_ref):
        send_ref[...] = tile_ref[1:, :, at_half(1 - core_ref[0], half_w)]

    (tiles_out,) = call(cut, [core], [by_step], [((STEPS - 1, frames, half_w), bf16)], name="cut")
    other_tiles = swap(tiles_out, "swap_tiles")

    def pick(core_ref, keep_ref, came_ref, even_ref, odd_ref):
        home = core_ref[0] == 0
        even_ref[...] = jnp.where(home, keep_ref[...], came_ref[...])
        odd_ref[...] = jnp.where(home, came_ref[...], keep_ref[...])

    even, odd = call(pick, [core], [keep, came], [payload_shape] * 2, name="pick")
    odd = hop(odd, "hop_odd0")

    def both(core_ref, own_ref, own_t_ref, other_ref, *outs):
        def lay(mine, mine_t, theirs, theirs_t):
            mine[...] = own_ref[...]
            mine_t[...] = own_t_ref[...]
            for at in range(0, frames, RUN_LEN):
                rows = slice(at, at + RUN_LEN)
                new = other_ref[rows, :]
                theirs[rows, :] = new
                theirs_t[:, rows] = new.T

        even_loads, even_t, odd_loads, odd_t = outs

        @pl.when(core_ref[0] == 0)
        def _():
            lay(even_loads, even_t, odd_loads, odd_t)

        @pl.when(core_ref[0] == 1)
        def _():
            lay(odd_loads, odd_t, even_loads, even_t)

    *even_l, odd_loads, odd_t = call(
        both, [core], [own, own_t, other], [loads_shape, loads_t_shape] * 2, name="both"
    )
    loads = [even_l, [odd_loads, odd_t]]

    def visits(payload, stops, name):
        def body(core_ref, counts_ref, counts_other_ref, payload_ref, tile_ref, tile_other_ref, *refs):
            sides = {}
            for i, side in enumerate(sorted({s for s, _ in stops})):
                sides[side] = refs[2 * i : 2 * i + 2]
            outs = refs[2 * len(sides) :]
            held = decode(payload_ref)
            for i, (side, step) in enumerate(stops):
                home = core_ref[0] == side

                def tile_rows(at):
                    mine = tile_ref[step, at, at_half(core_ref[0], half_w)]
                    return jnp.where(home, mine, tile_other_ref[step - 1, at, :])

                counts = [
                    jnp.where(home, counts_ref[run], counts_other_ref[run])
                    for run in range(frames // RUN_LEN)
                ]
                held = visit(
                    held, tile_rows, counts, *sides[side], outs[1 + 2 * i], outs[2 + 2 * i]
                )
            encode(held, into(outs[0]))

        arrays = [payload, by_step, other_tiles]
        for side in sorted({s for s, _ in stops}):
            arrays += loads[side]
        result = call(
            body,
            [core, run_counts, other_counts],
            arrays,
            [payload_shape] + [resid_shape, bb_shape] * len(stops),
            name=name,
        )
        return result[0], [tuple(result[1 + 2 * i : 3 + 2 * i]) for i in range(len(stops))]

    def add_up(accs, work, name):
        sides = sorted(work)
        pairs = [x for side in sides for pair in work[side] for x in pair]

        def body(*refs):
            outs = refs[len(pairs) + len(sides) :]
            at = 0
            for i, side in enumerate(sides):
                for _ in work[side]:
                    outs[i][...] += pull(refs[at], refs[at + 1])
                    at += 2

        arrays = pairs + [accs[side] for side in sides]
        result = call(
            body,
            [],
            arrays,
            [acc_shape] * len(sides),
            name=name,
            aliases={len(pairs) + i: i for i in range(len(sides))},
        )
        accs = list(accs)
        for side, new in zip(sides, result):
            accs[side] = new
        return accs

    even, [got_1] = visits(even, [(1, 1)], "even1")
    even = hop(even, "hop_even1")

    def first_sums(core_ref, resid_ref, bb_ref, resid_1_ref, bb_1_ref, even_ref, odd_ref):
        odd_ref[...] = pull(resid_1_ref, bb_1_ref)

        @pl.when(core_ref[0] == 0)
        def _():
            even_ref[...] = pull(resid_ref, bb_ref)

        @pl.when(core_ref[0] == 1)
        def _():
            even_ref[...] = jnp.zeros(even_ref.shape, f32)
            odd_ref[...] += pull(resid_ref, bb_ref)

    accs = call(
        first_sums, [core], [resid_0, bb_0, *got_1], [acc_shape, acc_shape], name="first_sums"
    )

    odd, got = visits(odd, [(0, 1), (1, 2)], "odd12")
    odd = hop(odd, "hop_odd2")
    accs = add_up(accs, {0: [got[0]], 1: [got[1]]}, "sums_odd12")
    even, got = visits(even, [(0, 2), (1, 3)], "even23")
    even = hop(even, "hop_even3")

    def share(side, pairs, name):
        def body(core_ref, *refs):
            out_ref, acc_ref = refs[-2:]
            for i in range(len(pairs)):
                acc_ref[...] += pull(refs[2 * i], refs[2 * i + 1])
            out_ref[...] = acc_ref[at_half(1 - core_ref[0], half_f), :].astype(bf16)

        arrays = [x for pair in pairs for x in pair] + [accs[side]]
        out, accs[side] = call(
            body, [core], arrays, [rows_shape, acc_shape], name=name, aliases={len(arrays): 1}
        )
        return swap(out, f"swap_{name}")

    def meet(side, near, name):
        def body(core_ref, acc_ref, near_ref, out_ref):
            own_rows = acc_ref[at_half(core_ref[0], half_f), :]
            out_ref[...] = (own_rows + near_ref[...].astype(f32)).astype(bf16)

        (out,) = call(body, [core], [accs[side], near], [rows_shape], name=name)
        return across(out, f"across_{name}")

    def update(side, near, far, name):
        def body(core_ref, acc_ref, near_ref, far_ref, loadings_ref, other_ref, out_ref):
            rows = at_half(core_ref[0], half_f)
            total = acc_ref[rows, :] + near_ref[...].astype(f32) + far_ref[...].astype(f32)
            old = jnp.where(core_ref[0] == side, loadings_ref[rows, :], other_ref[...])
            out_ref[...] = (old + factor * total).astype(bf16)

        (out,) = call(
            body, [core], [accs[side], near, far, loadings, other_rows], [rows_shape], name=name
        )
        return out, swap(out, f"swap_{name}")

    def renew(mine, theirs, name):
        def body(core_ref, mine_ref, theirs_ref, loads_ref, loads_t_ref):
            for part_ref, index in ((mine_ref, core_ref[0]), (theirs_ref, 1 - core_ref[0])):
                loads_ref[at_half(index, half_f), :] = part_ref[...]
                loads_t_ref[:, at_half(index, half_f)] = part_ref[...].T

        return call(body, [core], [mine, theirs], [loads_shape, loads_t_shape], name=name)

    odd_near = share(1, [got[1]], "share_odd")
    accs = add_up(accs, {0: [got[0]]}, "sums_even2")
    odd_far = meet(1, odd_near, "meet_odd")
    odd, [got] = visits(odd, [(0, 3)], "odd3")
    even_near = share(0, [got], "share_even")
    even_far = meet(0, even_near, "meet_even")

    mine, theirs = update(1, odd_near, odd_far, "update_odd")
    loads[1] = renew(mine, theirs, "renew_odd")
    odd, [got_4] = visits(odd, [(1, 4)], "odd4")
    odd = hop(odd, "hop_odd4")
    accs = add_up(accs, {1: [got_4]}, "sums_odd4")

    mine, theirs = update(0, even_near, even_far, "update_even")
    loads[0] = renew(mine, theirs, "renew_even")
    even, got_e = visits(even, [(0, 4), (1, 5)], "even45")
    even = hop(even, "hop_even5")
    odd, got_o = visits(odd, [(0, 5), (1, 6)], "odd56")
    odd = hop(odd, "hop_odd6")
    accs = add_up(
        accs, {0: [got_e[0], got_o[0]], 1: [got_e[1], got_o[1]]}, "sums_45_56"
    )
    even, got_e = visits(even, [(0, 6), (1, 7)], "even67")
    even = hop(even, "hop_even7")
    accs = add_up(accs, {0: [got_e[0]], 1: [got_e[1]]}, "sums_even67")
    odd, [got] = visits(odd, [(0, 7)], "odd7")

    def send_end(core_ref, resid_ref, bb_ref, even_in, odd_ref, out_ref, even_ref):
        even_ref[...] += pull(resid_ref, bb_ref)

        @pl.when(core_ref[0] == 0)
        def _():
            out_ref[...] = odd_ref[...].astype(bf16)

        @pl.when(core_ref[0] == 1)
        def _():
            out_ref[...] = even_ref[...].astype(bf16)

    out, accs[0] = call(
        send_end,
        [core],
        [*got, accs[0], accs[1]],
        [loads_shape, acc_shape],
        name="send_end",
        aliases={3: 1},
    )
    near = swap(out, "swap_end")

    def meet_end(core_ref, panel_ref, even_ref, odd_ref, near_ref, out_ref, sum_ref):
        def total(acc_ref, index):
            rows = at_half(index, half_f)
            return acc_ref[rows, :] + near_ref[rows, :].astype(f32)

        for side, acc_ref in enumerate((even_ref, odd_ref)):

            @pl.when(core_ref[0] == side)
            def _():
                out_ref[...] = total(acc_ref, 1 - panel_ref[0]).astype(bf16)
                sum_ref[...] = total(acc_ref, panel_ref[0])

    out, total = call(
        meet_end, [core, panel], [accs[0], accs[1], near], [rows_shape, ((half_f, rank), f32)], name="meet_end"
    )
    far = across(out, "across_end")

    def maps_send(core_ref, even_ref, odd_ref, out_ref):
        out_ref[...] = jnp.where(core_ref[0] == 0, odd_ref[...], even_ref[...])

    (out,) = call(maps_send, [core], [even, odd], [payload_shape], name="maps_send")
    came = swap(out, "swap_maps")

    def maps_end(core_ref, even_ref, odd_ref, came_ref, out_ref):
        @pl.when(core_ref[0] == 0)
        def _():
            out_ref[:half_w, :] = decode(even_ref).T
            out_ref[half_w:, :] = decode(came_ref).T

        @pl.when(core_ref[0] == 1)
        def _():
            out_ref[:half_w, :] = decode(came_ref).T
            out_ref[half_w:, :] = decode(odd_ref).T

    (maps_after,) = call(
        maps_end, [core], [even, odd, came], [((width, rank), f32)], name="maps_end"
    )

    def loads_end(panel_ref, loadings_ref, total_ref, far_ref, out_ref):
        old = loadings_ref[at_half(panel_ref[0], half_f), :]
        out_ref[...] = old + factor * (total_ref[...] + far_ref[...].astype(f32))

    (loadings_out,) = call(
        loads_end, [panel], [loadings, total, far], [((half_f, rank), f32)], name="loads_end"
    )
    return loadings_out, maps_after.reshape(maps.shape)


def solution(mesh):
    in_specs = (
        P("blk", "panel", None, None),
        P("blk", None),
        P("blk", "panel", None, None),
        P("blk"),
    )
    out_specs = (P(("blk", "panel"), None), P("blk", "panel", None, None))
    return jax.shard_map(
        per_device, mesh=mesh, in_specs=in_specs, out_specs=out_specs, check_vma=False
    )
```
